32 devices in a mesh: lat: 4 (over x, core), lon: 8 (over z, y).
Axes of the slice: x: 2, y: 2, z: 4, core: 2. Of those that a mesh axis runs over, the one named last changes fastest.
Arguments:
- ensemble: bfloat16 [1920, 32, 1024], P(('lat', 'lon')), may hold values from -48 to 48
- obs_interp: bfloat16 [4, 8, 64, 4, 128], P('lat', 'lon'), may hold values from 0.049804688 to 1
- obs_start: int32 [4, 8, 64, 128], P('lat', 'lon'), may hold values from 0 to 124
- obs_levels: bfloat16 [4, 8, 64, 24, 128], P('lat', 'lon'), may hold values from -1.25 to 1.25
- obs_values: float32 [4, 8, 64, 128], P('lat', 'lon'), may hold values from -40 to 40
- obs_weight: float32 [4, 8, 64, 128], P('lat', 'lon'), may hold values from 0.001953125 to 0.00390625
- obs_rows: int32 [4, 8, 64], P('lat', 'lon'), may hold values from 0 to 7
- obs_count: int32 [4, 8], P('lat', 'lon'), may hold values from 8 to 64, as said below
- local_mask: int32 [4, 8, 8, 9], P('lat', 'lon'), may hold values 0 or 1
Outputs:
- analysis: bfloat16 [80, 24, 32, 1024], P(None, None, 'lat', 'lon')
The draws below stay inside these ranges and needn't reach their ends.
Inputs may be any that keep to these rules, and one draw needn't show every extreme that they name: `obs_count`: blocks from this slot on are ignored; some tile has 64 live blocks.
All inputs are finite; a program needn't handle non-finite values. No bound on the sum of `local_mask` on one device may be relied on, other than what follows from the above.
Results may differ from the reference program's by a relative error of at most 0.005.
Values may be sent and summed in bfloat16 or wider, within the bound.
A program may use at most 64 MiB of HBM per device.

```python
import math
import jax
import jax.numpy as jnp
from jax import lax

K = 80
NF = 24
TLAT = 8
TLON = 128
OB = 128
STENCIL = 4
MAXB = 64
NS_ITERS = 6
LAT_TILES = 4
LON_TILES = 8
NY = 32
NX = 1024


def draw_ensemble(key, part):
    keys = jax.random.split(key, 3)
    common = jax.random.normal(keys[0], (NF, NY, NX), jnp.float32)
    spread = jnp.exp(jax.random.uniform(keys[1], (K, 1, 1, 1), jnp.float32, jnp.log(0.5), jnp.log(4.0)))
    noise = jax.random.normal(keys[2], (K, NF, NY, NX), jnp.float32)
    return (common[None] + spread * noise).reshape(K * NF, NY, NX).astype(jnp.bfloat16)


def draw_obs_count(key, part):
    keys = jax.random.split(key, 4)
    tile_total = LAT_TILES * LON_TILES
    lowest = MAXB // 8
    drawn = jax.random.randint(keys[0], (tile_total,), lowest, MAXB // 2 + 1)
    dense = jax.random.randint(keys[1], (tile_total,), 0, 8) == 0
    heavy = jax.random.randint(keys[2], (tile_total,), 3 * MAXB // 4, MAXB + 1)
    counts = jnp.where(dense, heavy, drawn)
    order = jax.random.permutation(keys[3], tile_total)
    counts = counts.at[order[0]].set(MAXB).at[order[1]].set(lowest)
    return counts.reshape(LAT_TILES, LON_TILES).astype(jnp.int32)


def touch_ends(array, own_key, low, largest):
    longest = array.shape.index(max(array.shape))
    spots = []
    for shift in (0, 1):
        where = [jax.random.randint(jax.random.fold_in(own_key, axis), (), 0, length) for axis, length in enumerate(array.shape)]
        where[longest] = (where[longest] + shift) % array.shape[longest]
        spots.append(tuple(where))
    return array.at[spots[0]].set(low).at[spots[1]].set(largest)


def steps_of(rng, extent, shards, least, top_value):
    def one(axis_at, blocks):
        draws = jax.random.uniform(jax.random.fold_in(jax.random.fold_in(rng, 6), axis_at), (blocks,), jnp.float32, least / len(shards), top_value / len(shards))
        return jnp.repeat(jnp.exp(draws), extent[axis_at] // blocks).reshape((-1,) + (1,) * (len(extent) - axis_at - 1))

    gain = one(*shards[0])
    for cut in shards[1:]:
        gain = gain * one(*cut)
    return gain


def centred(own_key, extent, scale, most, cuts=(), kind=jnp.bfloat16):
    gain = steps_of(own_key, extent, cuts, -0.22, 0.18) if cuts else 1.0
    values = jax.random.normal(own_key, extent, jnp.float32) * scale * gain
    return jnp.minimum(jnp.maximum(values, -most), most).astype(kind)


def setup_inputs(seed: int = 0) -> dict:
    streams_of = jax.random.split(jax.random.key(seed), 10)
    return {
        "ensemble": draw_ensemble(jax.random.fold_in(streams_of[9], 71), 0),
        "obs_interp": jnp.clip(0.049804688 + 0.9501953 * jax.random.uniform(streams_of[1], (LAT_TILES, LON_TILES, MAXB, STENCIL, OB), jnp.float32) ** steps_of(streams_of[1], (LAT_TILES, LON_TILES, MAXB, STENCIL, OB), ((0, 4), (1, 8)), -0.2, 0.2), 0.049804688, 1.0).astype(jnp.bfloat16),
        "obs_start": touch_ends(jax.random.randint(streams_of[2], (LAT_TILES, LON_TILES, MAXB, OB), 0, TLON - STENCIL + 1), jax.random.fold_in(streams_of[2], 1), 0, TLON - STENCIL).astype(jnp.int32),
        "obs_levels": centred(streams_of[3], (LAT_TILES, LON_TILES, MAXB, NF, OB), NF ** -0.5, 1.25, ((0, 4), (1, 8))),
        "obs_values": centred(streams_of[4], (LAT_TILES, LON_TILES, MAXB, OB), 8.0, 40.0, ((0, 4), (1, 8)), jnp.float32),
        "obs_weight": jnp.clip(jnp.exp(math.log(0.00390625) - 0.6931472 * jax.random.uniform(streams_of[5], (LAT_TILES, LON_TILES, MAXB, OB), jnp.float32) ** steps_of(streams_of[5], (LAT_TILES, LON_TILES, MAXB, OB), ((0, 4), (1, 8)), -0.2, 0.2)), 0.001953125, 0.00390625),
        "obs_rows": touch_ends(jax.random.randint(streams_of[6], (LAT_TILES, LON_TILES, MAXB), 0, TLAT), jax.random.fold_in(streams_of[6], 1), 0, TLAT - 1).astype(jnp.int32),
        "obs_count": draw_obs_count(jax.random.fold_in(streams_of[9], 71), 0),
        "local_mask": touch_ends((jax.random.randint(streams_of[8], (LAT_TILES, LON_TILES, TLAT, 9), 0, 4) < 3).astype(jnp.int32), jax.random.fold_in(streams_of[8], 1), 0, 1),
    }


HIGHEST_PRECISION = lax.Precision.HIGHEST

def stencil_matrix(weights, starts, width):
    columns = jnp.arange(width, dtype=jnp.int32)
    dense = jnp.zeros(starts.shape + (width,), jnp.float32)
    for offset in range(weights.shape[1]):
        hit = starts[:, :, None] + offset == columns[None, None, :]
        dense = dense + jnp.where(hit, weights[:, offset, :, None].astype(jnp.float32), jnp.float32(0.0))
    return dense

def tile_partial(tile_state, interp, starts, levels, values, weights, block_rows, live_count):
    picked = jnp.take(tile_state, block_rows, axis=2).astype(jnp.float32)
    dense = stencil_matrix(interp, starts, tile_state.shape[3])
    projected = jnp.einsum('kfjc,joc->kfjo', picked, dense, precision=HIGHEST_PRECISION)
    obs_ens = lax.optimization_barrier(jnp.sum(projected * jnp.transpose(levels.astype(jnp.float32), (1, 0, 2))[None], axis=1))
    obs_mean = lax.optimization_barrier(jnp.mean(obs_ens, axis=0))
    obs_dev = obs_ens - obs_mean
    innov = values - obs_mean
    is_live = jnp.arange(values.shape[0], dtype=jnp.int32)[:, None] < live_count
    live = jnp.where(is_live, weights, jnp.zeros_like(weights))
    members = obs_dev.shape[0]
    flat_dev = obs_dev.reshape(members, -1)
    paired = jnp.concatenate([flat_dev.T, innov.reshape(-1, 1)], axis=1)
    return jnp.dot(flat_dev * live.reshape(1, -1), paired, precision=HIGHEST_PRECISION)

def ensemble_transform(summed, members):
    identity = jnp.eye(members, dtype=jnp.float32)
    system = (members - 1) * identity + summed[:, :, :members]
    target = summed[:, :, members]
    scale = jnp.sqrt(lax.optimization_barrier(jnp.sum(system * system, axis=(1, 2))))
    root_term = system / scale[:, None, None]
    inverse = jnp.broadcast_to(identity, system.shape)
    for repeat in range(NS_ITERS):
        middle = 1.5 * identity - 0.5 * jnp.einsum('bij,bjk->bik', inverse, root_term, precision=HIGHEST_PRECISION)
        root_term = jnp.einsum('bij,bjk->bik', root_term, middle, precision=HIGHEST_PRECISION)
        inverse = jnp.einsum('bij,bjk->bik', middle, inverse, precision=HIGHEST_PRECISION)
    half_step = jnp.einsum('bij,bj->bi', inverse, target, precision=HIGHEST_PRECISION)
    shift_mean = jnp.einsum('bij,bj->bi', inverse, half_step, precision=HIGHEST_PRECISION) / scale[:, None]
    spread = jnp.sqrt(jnp.float32(members - 1)) * inverse / jnp.sqrt(scale)[:, None, None]
    return (spread + shift_mean[:, :, None]).astype(jnp.bfloat16)

def reference(ensemble, obs_interp, obs_start, obs_levels, obs_values, obs_weight, obs_rows, obs_count, local_mask):
    members = K
    fields = NF
    grid = ensemble.reshape(members, fields, TLAT * LAT_TILES, TLON * LON_TILES)
    tile_total = LAT_TILES * LON_TILES

    def tile_slice(tile_index):
        lat_index = (tile_index // LON_TILES).astype(jnp.int32)
        lon_index = (tile_index % LON_TILES).astype(jnp.int32)
        anchor = jnp.int32(0)
        block = lax.dynamic_slice(grid, (anchor, anchor, lat_index * TLAT, lon_index * TLON), (members, fields, TLAT, TLON))
        return (block, lat_index, lon_index)

    def one_partial(tile_index):
        block, lat_index, lon_index = tile_slice(tile_index)
        return tile_partial(block, obs_interp[lat_index, lon_index], obs_start[lat_index, lon_index], obs_levels[lat_index, lon_index], obs_values[lat_index, lon_index], obs_weight[lat_index, lon_index], obs_rows[lat_index, lon_index], obs_count[lat_index, lon_index])
    tile_ids = jnp.arange(tile_total, dtype=jnp.int32)
    partials = lax.map(one_partial, tile_ids).reshape(LAT_TILES, LON_TILES, members, members + 1)
    lon_stack = jnp.stack([jnp.roll(partials, 1, axis=1), partials, jnp.roll(partials, -1, axis=1)], axis=2)
    zero_row = jnp.zeros_like(lon_stack[:1])
    north_rows = jnp.concatenate([zero_row, lon_stack[:-1]], axis=0)
    south_rows = jnp.concatenate([lon_stack[1:], zero_row], axis=0)
    partner = ((jnp.arange(LON_TILES, dtype=jnp.int32) + LON_TILES // 2) % LON_TILES).astype(jnp.int32)
    north_pole = lon_stack[0][partner][:, ::-1]
    north_rows = north_rows.at[0].set(north_pole)
    slot_sums = jnp.stack([north_rows, lon_stack, south_rows], axis=2).reshape(LAT_TILES, LON_TILES, 9, members * (members + 1))

    def one_tile(tile_index):
        block, lat_index, lon_index = tile_slice(tile_index)
        slot_mask = local_mask[lat_index, lon_index].astype(jnp.float32)
        summed = jnp.dot(slot_mask, slot_sums[lat_index, lon_index], precision=HIGHEST_PRECISION).reshape(TLAT, members, members + 1)
        transform = ensemble_transform(summed, members)
        ens_mean = lax.optimization_barrier(jnp.sum(block.astype(jnp.float32), axis=0)) / members
        deviation = (block.astype(jnp.float32) - ens_mean).astype(jnp.bfloat16)
        deviation = lax.optimization_barrier(deviation)
        transform = lax.optimization_barrier(transform)
        update = jnp.einsum('kfbc,bkl->lfbc', deviation.astype(jnp.float32), transform.astype(jnp.float32), precision=HIGHEST_PRECISION)
        return (ens_mean[None] + update).astype(jnp.bfloat16)
    blocks = lax.map(one_tile, tile_ids).reshape(LAT_TILES, LON_TILES, members, fields, TLAT, TLON)
    return jnp.transpose(blocks, (2, 3, 0, 4, 1, 5)).reshape(members, fields, TLAT * LAT_TILES, TLON * LON_TILES)
```

```python
import functools
import math

import jax
import jax.numpy as jnp
from jax import lax
from jax.experimental import pallas as pl
from jax.experimental.pallas import tpu as pltpu
from jax.sharding import PartitionSpec as P

NS_ITERS = 6
MESH = pl.DeviceIdType.MESH
HIGHEST_PRECISION = lax.Precision.HIGHEST


def gather_kernel(
    plan,
    ens_ref,
    interp_ref,
    starts_ref,
    levels_ref,
    values_ref,
    weights_ref,
    rows_ref,
    count_ref,
    state_ref,
    slots_ref,
    dense,
    by_row,
    wide,
    obs,
    partial,
    send_sem,
    recv_sem,
    slot_send,
    slot_recv,
):
    lat_n, lon_n, share, tile_rows, tile_cols, levels_n, members, group = plan
    total = lat_n * lon_n
    halves = lon_n // group
    group_rows = group * share
    group_members = group_rows // levels_n
    padded_members = obs.shape[1] // (total // group)
    slots_n, stencil = interp_ref.shape[2:4]
    lat, lon = lax.axis_index("lat"), lax.axis_index("lon")
    me = lat * lon_n + lon
    half = lon // group

    barrier = pltpu.get_barrier_semaphore()

    @pl.loop(1, total)
    def _(step):
        peer = lax.rem(me + step, total)
        pl.semaphore_signal(
            barrier,
            inc=1,
            device_id={"lat": peer // lon_n, "lon": lax.rem(peer, lon_n)},
            device_id_type=MESH,
        )

    pl.semaphore_wait(barrier, total - 1)

    def tile_copy(to_lat, to_lon, source):
        return pltpu.make_async_remote_copy(
            src_ref=ens_ref.at[
                :,
                pl.ds(pl.multiple_of(to_lat * tile_rows, tile_rows), tile_rows),
                pl.ds(pl.multiple_of(to_lon * tile_cols, tile_cols), tile_cols),
            ],
            dst_ref=state_ref.at[pl.ds(source * share, share)],
            send_sem=send_sem.at[to_lat * lon_n + to_lon],
            recv_sem=recv_sem.at[source],
            device_id={"lat": to_lat, "lon": to_lon},
            device_id_type=MESH,
        )

    own = pltpu.make_async_copy(
        ens_ref.at[
            :,
            pl.ds(pl.multiple_of(lat * tile_rows, tile_rows), tile_rows),
            pl.ds(pl.multiple_of(lon * tile_cols, tile_cols), tile_cols),
        ],
        state_ref.at[pl.ds(me * share, share)],
        recv_sem.at[me],
    )
    own.start()
    reach = [u for u in range(1, halves)] + [0]

    @pl.loop(0, lat_n)
    def _(turn):
        to_lat = lax.rem(lat + lat_n - turn, lat_n)
        for u in reach:
            to_half = lax.rem(half + u, halves)

            @pl.loop(0, group)
            def _(i):
                to_lon = to_half * group + lax.rem(lon + i, group)

                @pl.when(to_lat * lon_n + to_lon != me)
                def _():
                    tile_copy(to_lat, to_lon, me).start()

    cells = lax.broadcasted_iota(jnp.int32, (tile_cols, starts_ref.shape[-1]), 0)

    @pl.loop(0, slots_n)
    def _(j):
        first = starts_ref[0, 0, pl.ds(j, 1), :]
        taps = interp_ref[0, 0, j].astype(jnp.float32)
        offset = cells - first
        grid = jnp.zeros(cells.shape, jnp.float32)
        for p in range(stencil):
            grid = jnp.where(offset == p, taps[p : p + 1, :], grid)
        dense[j] = grid.astype(jnp.bfloat16)

    def take_group(which):
        base = which * group_rows

        @pl.loop(0, group)
        def _(i):
            source = which * group + i
            tile_copy(source // lon_n, lax.rem(source, lon_n), source).wait_recv()

        @pl.loop(0, group_rows // 16)
        def _(i):
            piece = state_ref[pl.ds(base + i * 16, 16)].astype(jnp.float32)
            wide[pl.ds(pl.multiple_of(i * 16 * tile_rows, 16 * tile_rows), 16 * tile_rows), :] = (
                piece.reshape(16 * tile_rows, tile_cols)
            )

        for r in range(tile_rows):
            by_row[r] = wide[pl.ds(r, group_rows, stride=tile_rows), :].astype(jnp.bfloat16)

        @pl.loop(0, slots_n, unroll=4)
        def _(j):
            product = jnp.dot(by_row[rows_ref[j]], dense[j], preferred_element_type=jnp.float32)
            level = levels_ref[0, 0, j].astype(jnp.float32)
            folded = jnp.sum(
                product.reshape(group_members, levels_n, product.shape[1]) * level[None], axis=1
            )
            blank = jnp.zeros((padded_members - group_members, folded.shape[1]), jnp.float32)
            obs[j, pl.ds(pl.multiple_of(which * padded_members, 8), padded_members), :] = (
                jnp.concatenate([folded, blank], axis=0)
            )

    for u in range(halves):

        @pl.loop(0, lat_n)
        def _(turn):
            from_lat = lax.rem(lat + turn, lat_n)
            take_group(from_lat * halves + lax.rem(half + u, halves))

    span = obs.shape[1]
    row_ids = lax.broadcasted_iota(jnp.int32, (span, tile_cols), 0)
    real = lax.rem(row_ids, padded_members) < group_members

    def add_block(j, carry):
        block = obs[j]
        mean = jnp.sum(block, axis=0, keepdims=True) / members
        dev = jnp.where(real, block - mean, 0.0)
        innov = values_ref[0, 0, pl.ds(j, 1), :] - mean
        right = jnp.where(row_ids == group_members, innov, dev).astype(jnp.bfloat16)
        weight = weights_ref[0, 0, pl.ds(j, 1), :]
        live = jnp.where(jnp.full(weight.shape, j, jnp.int32) < count_ref[0], weight, 0.0)
        left = (dev * live).astype(jnp.bfloat16)
        return carry + lax.dot_general(
            left, right, (((1,), (1,)), ((), ())), preferred_element_type=jnp.float32
        )

    partial[...] = lax.fori_loop(
        0, slots_n, add_block, jnp.zeros((span, span), jnp.float32), unroll=4
    )

    def slot_copy(to_lat, to_lon, slot, out):
        return pltpu.make_async_remote_copy(
            src_ref=partial,
            dst_ref=slots_ref.at[slot],
            send_sem=slot_send.at[out],
            recv_sem=slot_recv.at[slot],
            device_id={"lat": to_lat, "lon": to_lon},
            device_id_type=MESH,
        )

    def away(distance):
        return lax.rem(lon + lon_n + distance, lon_n)

    last = lat_n - 1
    east_west = [slot_copy(lat, away(1), 3, 3), slot_copy(lat, away(-1), 5, 5)]
    south = [slot_copy(lat + 1, away(1 - s), s, s) for s in range(3)]
    north = [slot_copy(lat - 1, away(1 - s), 6 + s, 6 + s) for s in range(3)]
    pole = [slot_copy(lat, away(s - 1 - lon_n // 2), s, 6 + s) for s in range(3)]
    for copy in east_west:
        copy.start()

    @pl.when(lat < last)
    def _():
        for copy in south:
            copy.start()

    @pl.when(lat > 0)
    def _():
        for copy in north:
            copy.start()

    @pl.when(lat == 0)
    def _():
        for copy in pole:
            copy.start()

    slots_ref[4] = partial[...]

    @pl.when(lat == last)
    def _():
        for s in range(3):
            slots_ref[6 + s] = jnp.zeros((span, span), jnp.float32)

    @pl.loop(0, total)
    def _(peer):
        @pl.when(peer != me)
        def _():
            tile_copy(peer // lon_n, lax.rem(peer, lon_n), me).wait_send()

    for copy in east_west:
        copy.wait()
    for copy in pole:
        copy.wait_recv()
        copy.wait_send()

    @pl.when(lat < last)
    def _():
        for copy in south:
            copy.wait_send()
        for copy in north:
            copy.wait_recv()


def ensemble_transform(summed, members):
    identity = jnp.eye(members, dtype=jnp.float32)
    system = (members - 1) * identity + summed[:, :, :members]
    target = summed[:, :, members]
    scale = jnp.sqrt(jnp.sum(system * system, axis=(1, 2)))
    root_term = system / scale[:, None, None]
    inverse = jnp.broadcast_to(identity, system.shape)
    for repeat in range(NS_ITERS):
        middle = 1.5 * identity - 0.5 * jnp.einsum(
            "bij,bjk->bik", inverse, root_term, precision=HIGHEST_PRECISION
        )
        root_term = jnp.einsum("bij,bjk->bik", root_term, middle, precision=HIGHEST_PRECISION)
        inverse = jnp.einsum("bij,bjk->bik", middle, inverse, precision=HIGHEST_PRECISION)
    half_step = jnp.einsum("bij,bj->bi", inverse, target, precision=HIGHEST_PRECISION)
    shift_mean = (
        jnp.einsum("bij,bj->bi", inverse, half_step, precision=HIGHEST_PRECISION) / scale[:, None]
    )
    spread = jnp.sqrt(jnp.float32(members - 1)) * inverse / jnp.sqrt(scale)[:, None, None]
    return (spread + shift_mean[:, :, None]).astype(jnp.bfloat16)


def per_device(
    ensemble,
    obs_interp,
    obs_start,
    obs_levels,
    obs_values,
    obs_weight,
    obs_rows,
    obs_count,
    local_mask,
):
    lat_n = lax.axis_size("lat")
    lon_n = lax.axis_size("lon")
    total = lat_n * lon_n
    share, grid_rows, grid_cols = ensemble.shape
    tile_rows = grid_rows // lat_n
    tile_cols = grid_cols // lon_n
    slots_n, levels_n, obs_n = obs_levels.shape[2:]
    members = share * total // levels_n
    group = math.lcm(share, math.lcm(levels_n, 16)) // share
    groups = total // group
    group_members = group * share // levels_n
    padded_members = (group_members // 8 + 1) * 8
    span = groups * padded_members
    plan = (lat_n, lon_n, share, tile_rows, tile_cols, levels_n, members, group)
    vmem = pl.BlockSpec(memory_space=pltpu.VMEM)
    smem = pl.BlockSpec(memory_space=pltpu.SMEM)
    state, slots = pl.pallas_call(
        functools.partial(gather_kernel, plan),
        out_shape=(
            jax.ShapeDtypeStruct((share * total, tile_rows, tile_cols), jnp.bfloat16),
            jax.ShapeDtypeStruct((9, span, span), jnp.float32),
        ),
        in_specs=[pl.BlockSpec(memory_space=pl.ANY)] + [vmem] * 5 + [smem] * 2,
        out_specs=(vmem, vmem),
        scratch_shapes=[
            pltpu.VMEM((slots_n, tile_cols, obs_n), jnp.bfloat16),
            pltpu.VMEM((tile_rows, group * share, tile_cols), jnp.bfloat16),
            pltpu.VMEM((group * share * tile_rows, tile_cols), jnp.float32),
            pltpu.VMEM((slots_n, span, obs_n), jnp.float32),
            pltpu.VMEM((span, span), jnp.float32),
            pltpu.SemaphoreType.DMA((total,)),
            pltpu.SemaphoreType.DMA((total,)),
            pltpu.SemaphoreType.DMA((9,)),
            pltpu.SemaphoreType.DMA((9,)),
        ],
        compiler_params=pltpu.CompilerParams(
            collective_id=0, has_side_effects=True, vmem_limit_bytes=40 * 1024 * 1024
        ),
    )(
        ensemble,
        obs_interp,
        obs_start,
        obs_levels,
        obs_values,
        obs_weight,
        obs_rows.reshape(-1),
        obs_count.reshape(-1),
    )
    tile_state = state.reshape(members, levels_n, tile_rows, tile_cols)
    ens_mean = jnp.sum(tile_state, axis=0, dtype=jnp.float32) / members
    deviation = (tile_state - ens_mean).astype(jnp.bfloat16)
    slot_mask = local_mask[0, 0].astype(jnp.float32)
    spread = jnp.dot(slot_mask, slots.reshape(9, span * span), precision=HIGHEST_PRECISION)
    spread = spread.reshape(tile_rows, groups, padded_members, groups, padded_members)
    system = spread[:, :, :group_members, :, :group_members].reshape(tile_rows, members, members)
    target = spread[:, :, :group_members, 0, group_members].reshape(tile_rows, members, 1)
    transform = ensemble_transform(jnp.concatenate([system, target], axis=2), members)
    update = jnp.einsum("kfbc,bkl->lfbc", deviation, transform, preferred_element_type=jnp.float32)
    return (ens_mean[None] + update).astype(jnp.bfloat16)


def solution(mesh):
    placed = (
        P(("lat", "lon"), None, None),
        P("lat", "lon", None, None, None),
        P("lat", "lon", None, None),
        P("lat", "lon", None, None, None),
        P("lat", "lon", None, None),
        P("lat", "lon", None, None),
        P("lat", "lon", None),
        P("lat", "lon"),
        P("lat", "lon", None, None),
    )
    return jax.shard_map(
        per_device,
        mesh=mesh,
        in_specs=placed,
        out_specs=P(None, None, "lat", "lon"),
        check_vma=False,
    )
```

```python
import functools
import math

import jax
import jax.numpy as jnp
from jax import lax
from jax.experimental import pallas as pl
from jax.experimental.pallas import tpu as pltpu
from jax.sharding import PartitionSpec as P

NS_ITERS = 6
MESH = pl.DeviceIdType.MESH


def gather_kernel(
    plan,
    ens_ref,
    interp_in,
    starts_in,
    levels_in,
    values_in,
    weights_in,
    rows_ref,
    count_ref,
    state_ref,
    slots_ref,
    interp_ref,
    starts_ref,
    levels_ref,
    values_ref,
    weights_ref,
    dense,
    by_row,
    wide,
    obs,
    partial,
    send_sem,
    recv_sem,
    slot_send,
    slot_recv,
    load_sem,
):
    lat_n, lon_n, share, tile_rows, tile_cols, levels_n, members, group = plan
    total = lat_n * lon_n
    halves = lon_n // group
    group_rows = group * share
    group_members = group_rows // levels_n
    padded_members = obs.shape[1] // (total // group)
    slots_n, stencil = interp_ref.shape[2:4]
    lat, lon = lax.axis_index("lat"), lax.axis_index("lon")
    me = lat * lon_n + lon
    half = lon // group

    barrier = pltpu.get_barrier_semaphore()

    @pl.loop(1, total)
    def _(step):
        peer = lax.rem(me + step, total)
        pl.semaphore_signal(
            barrier,
            inc=1,
            device_id={"lat": peer // lon_n, "lon": lax.rem(peer, lon_n)},
            device_id_type=MESH,
        )

    pl.semaphore_wait(barrier, total - 1)

    def tile_copy(to_lat, to_lon, source):
        return pltpu.make_async_remote_copy(
            src_ref=ens_ref.at[
                :,
                pl.ds(pl.multiple_of(to_lat * tile_rows, tile_rows), tile_rows),
                pl.ds(pl.multiple_of(to_lon * tile_cols, tile_cols), tile_cols),
            ],
            dst_ref=state_ref.at[pl.ds(source * share, share)],
            send_sem=send_sem.at[to_lat * lon_n + to_lon],
            recv_sem=recv_sem.at[source],
            device_id={"lat": to_lat, "lon": to_lon},
            device_id_type=MESH,
        )

    own = pltpu.make_async_copy(
        ens_ref.at[
            :,
            pl.ds(pl.multiple_of(lat * tile_rows, tile_rows), tile_rows),
            pl.ds(pl.multiple_of(lon * tile_cols, tile_cols), tile_cols),
        ],
        state_ref.at[pl.ds(me * share, share)],
        recv_sem.at[me],
    )
    own.start()
    reach = [u for u in range(1, halves)] + [0]

    @pl.loop(0, lat_n)
    def _(turn):
        to_lat = lax.rem(lat + lat_n - turn, lat_n)
        for u in reach:
            to_half = lax.rem(half + u, halves)

            @pl.loop(0, group)
            def _(i):
                to_lon = to_half * group + lax.rem(lon + i, group)

                @pl.when(to_lat * lon_n + to_lon != me)
                def _():
                    tile_copy(to_lat, to_lon, me).start()

    loads = [
        pltpu.make_async_copy(source, target, load_sem.at[i])
        for i, (source, target) in enumerate(
            [
                (interp_in, interp_ref),
                (starts_in, starts_ref),
                (levels_in, levels_ref),
                (values_in, values_ref),
                (weights_in, weights_ref),
            ]
        )
    ]
    for copy in loads:
        copy.start()
    for copy in loads:
        copy.wait()

    cells = lax.broadcasted_iota(jnp.int32, (tile_cols, starts_ref.shape[-1]), 0)

    @pl.loop(0, slots_n)
    def _(j):
        first = starts_ref[0, 0, pl.ds(j, 1), :]
        taps = interp_ref[0, 0, j].astype(jnp.float32)
        offset = cells - first
        grid = jnp.zeros(cells.shape, jnp.float32)
        for p in range(stencil):
            grid = jnp.where(offset == p, taps[p : p + 1, :], grid)
        dense[j] = grid.astype(jnp.bfloat16)

    def take_group(which):
        base = which * group_rows

        @pl.loop(0, group)
        def _(i):
            source = which * group + i
            tile_copy(source // lon_n, lax.rem(source, lon_n), source).wait_recv()

        @pl.loop(0, group_rows // 16)
        def _(i):
            piece = state_ref[pl.ds(base + i * 16, 16)].astype(jnp.float32)
            wide[pl.ds(pl.multiple_of(i * 16 * tile_rows, 16 * tile_rows), 16 * tile_rows), :] = (
                piece.reshape(16 * tile_rows, tile_cols)
            )

        for r in range(tile_rows):
            by_row[r] = wide[pl.ds(r, group_rows, stride=tile_rows), :].astype(jnp.bfloat16)

        @pl.loop(0, slots_n, unroll=4)
        def _(j):
            product = jnp.dot(by_row[rows_ref[j]], dense[j], preferred_element_type=jnp.float32)
            level = levels_ref[0, 0, j].astype(jnp.float32)
            folded = jnp.sum(
                product.reshape(group_members, levels_n, product.shape[1]) * level[None], axis=1
            )
            blank = jnp.zeros((padded_members - group_members, folded.shape[1]), jnp.float32)
            obs[j, pl.ds(pl.multiple_of(which * padded_members, 8), padded_members), :] = (
                jnp.concatenate([folded, blank], axis=0)
            )

    for u in range(halves):

        @pl.loop(0, lat_n)
        def _(turn):
            from_lat = lax.rem(lat + turn, lat_n)
            take_group(from_lat * halves + lax.rem(half + u, halves))

    span = obs.shape[1]
    row_ids = lax.broadcasted_iota(jnp.int32, (span, tile_cols), 0)
    real = lax.rem(row_ids, padded_members) < group_members

    def add_block(j, carry):
        block = obs[j]
        mean = jnp.sum(block, axis=0, keepdims=True) / members
        dev = jnp.where(real, block - mean, 0.0)
        innov = values_ref[0, 0, pl.ds(j, 1), :] - mean
        right = jnp.where(row_ids == group_members, innov, dev).astype(jnp.bfloat16)
        weight = weights_ref[0, 0, pl.ds(j, 1), :]
        live = jnp.where(jnp.full(weight.shape, j, jnp.int32) < count_ref[0], weight, 0.0)
        left = (dev * live).astype(jnp.bfloat16)
        return carry + lax.dot_general(
            left, right, (((1,), (1,)), ((), ())), preferred_element_type=jnp.float32
        )

    partial[...] = lax.fori_loop(
        0, slots_n, add_block, jnp.zeros((span, span), jnp.float32), unroll=4
    )

    def slot_copy(to_lat, to_lon, slot, out):
        return pltpu.make_async_remote_copy(
            src_ref=partial,
            dst_ref=slots_ref.at[slot],
            send_sem=slot_send.at[out],
            recv_sem=slot_recv.at[slot],
            device_id={"lat": to_lat, "lon": to_lon},
            device_id_type=MESH,
        )

    def away(distance):
        return lax.rem(lon + lon_n + distance, lon_n)

    last = lat_n - 1
    east_west = [slot_copy(lat, away(1), 3, 3), slot_copy(lat, away(-1), 5, 5)]
    south = [slot_copy(lat + 1, away(1 - s), s, s) for s in range(3)]
    north = [slot_copy(lat - 1, away(1 - s), 6 + s, 6 + s) for s in range(3)]
    pole = [slot_copy(lat, away(s - 1 - lon_n // 2), s, 6 + s) for s in range(3)]
    for copy in east_west:
        copy.start()

    @pl.when(lat < last)
    def _():
        for copy in south:
            copy.start()

    @pl.when(lat > 0)
    def _():
        for copy in north:
            copy.start()

    @pl.when(lat == 0)
    def _():
        for copy in pole:
            copy.start()

    slots_ref[4] = partial[...]

    @pl.when(lat == last)
    def _():
        for s in range(3):
            slots_ref[6 + s] = jnp.zeros((span, span), jnp.float32)

    @pl.loop(0, total)
    def _(peer):
        @pl.when(peer != me)
        def _():
            tile_copy(peer // lon_n, lax.rem(peer, lon_n), me).wait_send()

    for copy in east_west:
        copy.wait()
    for copy in pole:
        copy.wait_recv()
        copy.wait_send()

    @pl.when(lat < last)
    def _():
        for copy in south:
            copy.wait_send()
        for copy in north:
            copy.wait_recv()


def split_dot(left, right):
    left_high = left.astype(jnp.bfloat16)
    left_low = (left - left_high.astype(jnp.float32)).astype(jnp.bfloat16)
    right_high = right.astype(jnp.bfloat16)
    right_low = (right - right_high.astype(jnp.float32)).astype(jnp.bfloat16)
    return jnp.dot(
        jnp.concatenate([left_high, left_high, left_low], axis=1),
        jnp.concatenate([right_high, right_low, right_high], axis=0),
        preferred_element_type=jnp.float32,
    )


def analysis_kernel(
    plan,
    state_ref,
    slots_ref,
    mask_ref,
    out_ref,
    root,
    inverse,
    target,
    scales,
    wide,
    big,
    dev,
    mean,
    result,
    out_sem,
):
    members, levels_n, tile_rows, tile_cols, group_members, padded_members, ns_iters = plan
    span = slots_ref.shape[1]
    deep = members * tile_rows
    rows = lax.broadcasted_iota(jnp.int32, (span, span), 0)
    cols = lax.broadcasted_iota(jnp.int32, (span, span), 1)
    real_cols = lax.rem(cols, padded_members) < group_members
    identity = jnp.where((rows == cols) & real_cols, 1.0, 0.0)

    @pl.loop(0, tile_rows)
    def _(b):
        summed = mask_ref[b * 9].astype(jnp.float32) * slots_ref[0]
        for slot in range(1, 9):
            summed += mask_ref[b * 9 + slot].astype(jnp.float32) * slots_ref[slot]
        system = (members - 1) * identity + jnp.where(real_cols, summed, 0.0)
        total = jnp.sum(jnp.sum(system * system, axis=0, keepdims=True), axis=1, keepdims=True)
        scale = jnp.sqrt(total)
        scales[b] = jnp.broadcast_to(scale, scales.shape[1:])
        target[b] = jnp.sum(
            jnp.where(cols == group_members, summed, 0.0), axis=1, keepdims=True
        )
        root_term = system / scale
        middle = 1.5 * identity - 0.5 * root_term
        root[b] = split_dot(root_term, middle)
        inverse[b] = middle

    @pl.loop(0, levels_n)
    def _(f):
        cell = state_ref[:, f].astype(jnp.float32)
        average = jnp.sum(cell, axis=0) / members
        mean[f] = average
        dev[f] = (cell - average[None]).reshape(deep, tile_cols).astype(jnp.bfloat16)

    @pl.loop(0, ns_iters - 2)
    def _(repeat):
        for b in range(tile_rows):
            root_term, term = root[b], inverse[b]
            middle = 1.5 * identity - 0.5 * split_dot(term, root_term)
            root[b] = split_dot(root_term, middle)
            inverse[b] = split_dot(middle, term)

    chosen = lax.broadcasted_iota(jnp.int32, (members, span), 0)
    place = lax.broadcasted_iota(jnp.int32, (members, span), 1)
    picked = (place // padded_members) * group_members + lax.rem(place, padded_members)
    pick = jnp.where(
        (picked == chosen) & (lax.rem(place, padded_members) < group_members), 1.0, 0.0
    ).astype(jnp.bfloat16)
    source = lax.broadcasted_iota(jnp.int32, (span, deep), 0)
    spot = lax.broadcasted_iota(jnp.int32, (span, deep), 1)
    member_of = (source // padded_members) * group_members + lax.rem(source, padded_members)
    spot = jnp.where(
        lax.rem(source, padded_members) < group_members, spot - member_of * tile_rows, -1
    )

    for b in range(tile_rows):
        term = inverse[b]
        middle = 1.5 * identity - 0.5 * split_dot(term, root[b])
        term = split_dot(middle, term)
        scale = scales[b][:1, :1]
        half_step = jnp.sum(term * target[b], axis=0, keepdims=True)
        shift = jnp.sum(term * half_step, axis=1, keepdims=True) / scale
        spread = jnp.sqrt(jnp.float32(members - 1)) * term / jnp.sqrt(scale)
        transform = (spread + shift).astype(jnp.bfloat16)
        turned = lax.dot_general(
            pick, transform, (((1,), (1,)), ((), ())), preferred_element_type=jnp.float32
        ).astype(jnp.bfloat16)
        spread_out = jnp.dot(
            turned,
            jnp.where(spot == b, 1.0, 0.0).astype(jnp.bfloat16),
            preferred_element_type=jnp.float32,
        )
        for part in range(deep // tile_cols):
            wide[part, pl.ds(b, members, stride=tile_rows), :] = spread_out[
                :, part * tile_cols : (part + 1) * tile_cols
            ]

    for part in range(deep // tile_cols):
        big[:, part * tile_cols : (part + 1) * tile_cols] = wide[part].astype(jnp.bfloat16)

    def send(pair):
        return pltpu.make_async_copy(
            result.at[:, pl.ds(pair * 2, 2)], out_ref.at[:, pl.ds(pair * 2, 2)], out_sem.at[pair]
        )

    chunk = 128

    @pl.loop(0, levels_n // 2)
    def _(pair):
        f = pair * 2
        right = jnp.concatenate([dev[f], dev[f + 1]], axis=1)
        averages = [mean[f], mean[f + 1]]
        for first in range(0, deep, chunk):
            update = jnp.dot(
                big[first : first + chunk, :], right, preferred_element_type=jnp.float32
            )
            for half in range(2):
                block = update[:, half * tile_cols : (half + 1) * tile_cols].reshape(
                    chunk // tile_rows, tile_rows, tile_cols
                )
                result[first // tile_rows : (first + chunk) // tile_rows, f + half] = (
                    block + averages[half][None]
                ).astype(jnp.bfloat16)
        send(pair).start()

    @pl.loop(0, levels_n // 2)
    def _(pair):
        send(pair).wait()


def per_device(
    ensemble,
    obs_interp,
    obs_start,
    obs_levels,
    obs_values,
    obs_weight,
    obs_rows,
    obs_count,
    local_mask,
):
    lat_n = lax.axis_size("lat")
    lon_n = lax.axis_size("lon")
    total = lat_n * lon_n
    share, grid_rows, grid_cols = ensemble.shape
    tile_rows = grid_rows // lat_n
    tile_cols = grid_cols // lon_n
    slots_n, levels_n, obs_n = obs_levels.shape[2:]
    members = share * total // levels_n
    group = math.lcm(share, math.lcm(levels_n, 16)) // share
    groups = total // group
    group_members = group * share // levels_n
    padded_members = (group_members // 8 + 1) * 8
    span = groups * padded_members
    plan = (lat_n, lon_n, share, tile_rows, tile_cols, levels_n, members, group)
    vmem = pl.BlockSpec(memory_space=pltpu.VMEM)
    smem = pl.BlockSpec(memory_space=pltpu.SMEM)
    state, slots = pl.pallas_call(
        functools.partial(gather_kernel, plan),
        out_shape=(
            jax.ShapeDtypeStruct((share * total, tile_rows, tile_cols), jnp.bfloat16),
            jax.ShapeDtypeStruct((9, span, span), jnp.float32),
        ),
        in_specs=[pl.BlockSpec(memory_space=pltpu.HBM)] * 6 + [smem] * 2,
        out_specs=(vmem, vmem),
        scratch_shapes=[
            pltpu.VMEM(array.shape, array.dtype)
            for array in (obs_interp, obs_start, obs_levels, obs_values, obs_weight)
        ]
        + [
            pltpu.VMEM((slots_n, tile_cols, obs_n), jnp.bfloat16),
            pltpu.VMEM((tile_rows, group * share, tile_cols), jnp.bfloat16),
            pltpu.VMEM((group * share * tile_rows, tile_cols), jnp.float32),
            pltpu.VMEM((slots_n, span, obs_n), jnp.float32),
            pltpu.VMEM((span, span), jnp.float32),
            pltpu.SemaphoreType.DMA((total,)),
            pltpu.SemaphoreType.DMA((total,)),
            pltpu.SemaphoreType.DMA((9,)),
            pltpu.SemaphoreType.DMA((9,)),
            pltpu.SemaphoreType.DMA((5,)),
        ],
        compiler_params=pltpu.CompilerParams(
            collective_id=0, has_side_effects=True, vmem_limit_bytes=54 * 1024 * 1024
        ),
    )(
        ensemble,
        obs_interp,
        obs_start,
        obs_levels,
        obs_values,
        obs_weight,
        obs_rows.reshape(-1),
        obs_count.reshape(-1),
    )
    tile_state = state.reshape(members, levels_n, tile_rows, tile_cols)
    tiles = (tile_rows, span, span)
    deep = members * tile_rows
    plan = (members, levels_n, tile_rows, tile_cols, group_members, padded_members, NS_ITERS)
    return pl.pallas_call(
        functools.partial(analysis_kernel, plan),
        out_shape=jax.ShapeDtypeStruct(tile_state.shape, jnp.bfloat16),
        in_specs=[vmem, vmem, smem],
        out_specs=pl.BlockSpec(memory_space=pltpu.HBM),
        scratch_shapes=[
            pltpu.VMEM(tiles, jnp.float32),
            pltpu.VMEM(tiles, jnp.float32),
            pltpu.VMEM((tile_rows, span, 1), jnp.float32),
            pltpu.VMEM((tile_rows, 8, 128), jnp.float32),
            pltpu.VMEM((deep // tile_cols, deep, tile_cols), jnp.float32),
            pltpu.VMEM((deep, deep), jnp.bfloat16),
            pltpu.VMEM((levels_n, deep, tile_cols), jnp.bfloat16),
            pltpu.VMEM((levels_n, tile_rows, tile_cols), jnp.float32),
            pltpu.VMEM(tile_state.shape, jnp.bfloat16),
            pltpu.SemaphoreType.DMA((levels_n // 2,)),
        ],
        compiler_params=pltpu.CompilerParams(vmem_limit_bytes=40 * 1024 * 1024),
    )(tile_state, slots, local_mask.reshape(-1))


def solution(mesh):
    placed = (
        P(("lat", "lon"), None, None),
        P("lat", "lon", None, None, None),
        P("lat", "lon", None, None),
        P("lat", "lon", None, None, None),
        P("lat", "lon", None, None),
        P("lat", "lon", None, None),
        P("lat", "lon", None),
        P("lat", "lon"),
        P("lat", "lon", None, None),
    )
    return jax.shard_map(
        per_device,
        mesh=mesh,
        in_specs=placed,
        out_specs=P(None, None, "lat", "lon"),
        check_vma=False,
    )
```

```python
import functools
import math

import jax
import jax.numpy as jnp
from jax import lax
from jax.experimental import pallas as pl
from jax.experimental.pallas import tpu as pltpu
from jax.sharding import PartitionSpec as P

NS_ITERS = 6
MESH = pl.DeviceIdType.MESH


def gather_kernel(
    plan,
    ens_ref,
    interp_in,
    starts_in,
    levels_in,
    values_in,
    weights_in,
    rows_ref,
    count_ref,
    state_ref,
    slots_ref,
    interp_ref,
    starts_ref,
    levels_ref,
    values_ref,
    weights_ref,
    dense,
    by_row,
    wide,
    obs,
    partial,
    send_sem,
    recv_sem,
    slot_send,
    slot_recv,
    load_sem,
):
    lat_n, lon_n, share, tile_rows, tile_cols, levels_n, members, group = plan
    total = lat_n * lon_n
    halves = lon_n // group
    group_rows = group * share
    group_members = group_rows // levels_n
    padded_members = obs.shape[1] // (total // group)
    slots_n, stencil = interp_ref.shape[2:4]
    lat, lon = lax.axis_index("lat"), lax.axis_index("lon")
    me = lat * lon_n + lon
    half = lon // group

    barrier = pltpu.get_barrier_semaphore()

    @pl.loop(1, total)
    def _(step):
        peer = lax.rem(me + step, total)
        pl.semaphore_signal(
            barrier,
            inc=1,
            device_id={"lat": peer // lon_n, "lon": lax.rem(peer, lon_n)},
            device_id_type=MESH,
        )

    pl.semaphore_wait(barrier, total - 1)

    def tile_copy(to_lat, to_lon, source):
        return pltpu.make_async_remote_copy(
            src_ref=ens_ref.at[
                :,
                pl.ds(pl.multiple_of(to_lat * tile_rows, tile_rows), tile_rows),
                pl.ds(pl.multiple_of(to_lon * tile_cols, tile_cols), tile_cols),
            ],
            dst_ref=state_ref.at[pl.ds(source * share, share)],
            send_sem=send_sem.at[to_lat * lon_n + to_lon],
            recv_sem=recv_sem.at[source],
            device_id={"lat": to_lat, "lon": to_lon},
            device_id_type=MESH,
        )

    own = pltpu.make_async_copy(
        ens_ref.at[
            :,
            pl.ds(pl.multiple_of(lat * tile_rows, tile_rows), tile_rows),
            pl.ds(pl.multiple_of(lon * tile_cols, tile_cols), tile_cols),
        ],
        state_ref.at[pl.ds(me * share, share)],
        recv_sem.at[me],
    )
    own.start()
    reach = [u for u in range(1, halves)] + [0]

    @pl.loop(0, lat_n)
    def _(turn):
        to_lat = lax.rem(lat + lat_n - turn, lat_n)
        for u in reach:
            to_half = lax.rem(half + u, halves)

            @pl.loop(0, group)
            def _(i):
                to_lon = to_half * group + lax.rem(lon + i, group)

                @pl.when(to_lat * lon_n + to_lon != me)
                def _():
                    tile_copy(to_lat, to_lon, me).start()

    loads = [
        pltpu.make_async_copy(source, target, load_sem.at[i])
        for i, (source, target) in enumerate(
            [
                (interp_in, interp_ref),
                (starts_in, starts_ref),
                (levels_in, levels_ref),
                (values_in, values_ref),
                (weights_in, weights_ref),
            ]
        )
    ]
    for copy in loads:
        copy.start()
    for copy in loads:
        copy.wait()

    cells = lax.broadcasted_iota(jnp.int32, (tile_cols, starts_ref.shape[-1]), 0)

    @pl.loop(0, slots_n)
    def _(j):
        first = starts_ref[0, 0, pl.ds(j, 1), :]
        taps = interp_ref[0, 0, j].astype(jnp.float32)
        offset = cells - first
        grid = jnp.zeros(cells.shape, jnp.float32)
        for p in range(stencil):
            grid = jnp.where(offset == p, taps[p : p + 1, :], grid)
        dense[j] = grid.astype(jnp.bfloat16)

    def take_group(which):
        base = which * group_rows

        @pl.loop(0, group)
        def _(i):
            source = which * group + i
            tile_copy(source // lon_n, lax.rem(source, lon_n), source).wait_recv()

        @pl.loop(0, group_rows // 16)
        def _(i):
            piece = state_ref[pl.ds(base + i * 16, 16)].astype(jnp.float32)
            wide[pl.ds(pl.multiple_of(i * 16 * tile_rows, 16 * tile_rows), 16 * tile_rows), :] = (
                piece.reshape(16 * tile_rows, tile_cols)
            )

        for r in range(tile_rows):
            by_row[r] = wide[pl.ds(r, group_rows, stride=tile_rows), :].astype(jnp.bfloat16)

        @pl.loop(0, slots_n, unroll=4)
        def _(j):
            product = jnp.dot(by_row[rows_ref[j]], dense[j], preferred_element_type=jnp.float32)
            level = levels_ref[0, 0, j].astype(jnp.float32)
            folded = jnp.sum(
                product.reshape(group_members, levels_n, product.shape[1]) * level[None], axis=1
            )
            blank = jnp.zeros((padded_members - group_members, folded.shape[1]), jnp.float32)
            obs[j, pl.ds(pl.multiple_of(which * padded_members, 8), padded_members), :] = (
                jnp.concatenate([folded, blank], axis=0)
            )

    for u in range(halves):

        @pl.loop(0, lat_n)
        def _(turn):
            from_lat = lax.rem(lat + turn, lat_n)
            take_group(from_lat * halves + lax.rem(half + u, halves))

    span = obs.shape[1]
    row_ids = lax.broadcasted_iota(jnp.int32, (span, tile_cols), 0)
    real = lax.rem(row_ids, padded_members) < group_members

    def add_block(j, carry):
        block = obs[j]
        mean = jnp.sum(block, axis=0, keepdims=True) / members
        dev = jnp.where(real, block - mean, 0.0)
        innov = values_ref[0, 0, pl.ds(j, 1), :] - mean
        right = jnp.where(row_ids == group_members, innov, dev).astype(jnp.bfloat16)
        weight = weights_ref[0, 0, pl.ds(j, 1), :]
        live = jnp.where(jnp.full(weight.shape, j, jnp.int32) < count_ref[0], weight, 0.0)
        left = (dev * live).astype(jnp.bfloat16)
        return carry + lax.dot_general(
            left, right, (((1,), (1,)), ((), ())), preferred_element_type=jnp.float32
        )

    partial[...] = lax.fori_loop(
        0, slots_n, add_block, jnp.zeros((span, span), jnp.float32), unroll=4
    )

    def slot_copy(to_lat, to_lon, slot, out):
        return pltpu.make_async_remote_copy(
            src_ref=partial,
            dst_ref=slots_ref.at[slot],
            send_sem=slot_send.at[out],
            recv_sem=slot_recv.at[slot],
            device_id={"lat": to_lat, "lon": to_lon},
            device_id_type=MESH,
        )

    def away(distance):
        return lax.rem(lon + lon_n + distance, lon_n)

    last = lat_n - 1
    east_west = [slot_copy(lat, away(1), 3, 3), slot_copy(lat, away(-1), 5, 5)]
    south = [slot_copy(lat + 1, away(1 - s), s, s) for s in range(3)]
    north = [slot_copy(lat - 1, away(1 - s), 6 + s, 6 + s) for s in range(3)]
    pole = [slot_copy(lat, away(s - 1 - lon_n // 2), s, 6 + s) for s in range(3)]
    for copy in east_west:
        copy.start()

    @pl.when(lat < last)
    def _():
        for copy in south:
            copy.start()

    @pl.when(lat > 0)
    def _():
        for copy in north:
            copy.start()

    @pl.when(lat == 0)
    def _():
        for copy in pole:
            copy.start()

    slots_ref[4] = partial[...]

    @pl.when(lat == last)
    def _():
        for s in range(3):
            slots_ref[6 + s] = jnp.zeros((span, span), jnp.float32)

    @pl.loop(0, total)
    def _(peer):
        @pl.when(peer != me)
        def _():
            tile_copy(peer // lon_n, lax.rem(peer, lon_n), me).wait_send()

    for copy in east_west:
        copy.wait()
    for copy in pole:
        copy.wait_recv()
        copy.wait_send()

    @pl.when(lat < last)
    def _():
        for copy in south:
            copy.wait_send()
        for copy in north:
            copy.wait_recv()


def split_dot(left, right):
    left_high = left.astype(jnp.bfloat16)
    left_low = (left - left_high.astype(jnp.float32)).astype(jnp.bfloat16)
    right_high = right.astype(jnp.bfloat16)
    right_low = (right - right_high.astype(jnp.float32)).astype(jnp.bfloat16)
    return jnp.dot(
        jnp.concatenate([left_high, left_high, left_low], axis=1),
        jnp.concatenate([right_high, right_low, right_high], axis=0),
        preferred_element_type=jnp.float32,
    )


def analysis_kernel(
    plan,
    state_ref,
    slots_ref,
    mask_ref,
    out_ref,
    root,
    inverse,
    target,
    scales,
    wide,
    big,
    dev,
    mean,
    result,
    out_sem,
):
    members, levels_n, tile_rows, tile_cols, group_members, padded_members, ns_iters = plan
    span = slots_ref.shape[1]
    deep = members * tile_rows
    rows = lax.broadcasted_iota(jnp.int32, (span, span), 0)
    cols = lax.broadcasted_iota(jnp.int32, (span, span), 1)
    real_cols = lax.rem(cols, padded_members) < group_members
    identity = jnp.where((rows == cols) & real_cols, 1.0, 0.0)

    @pl.loop(0, tile_rows, unroll=4)
    def _(b):
        summed = mask_ref[b * 9].astype(jnp.float32) * slots_ref[0]
        for slot in range(1, 9):
            summed += mask_ref[b * 9 + slot].astype(jnp.float32) * slots_ref[slot]
        system = (members - 1) * identity + jnp.where(real_cols, summed, 0.0)
        total = jnp.sum(jnp.sum(system * system, axis=0, keepdims=True), axis=1, keepdims=True)
        scale = jnp.sqrt(total)
        scales[b] = jnp.broadcast_to(scale, scales.shape[1:])
        target[b] = jnp.sum(
            jnp.where(cols == group_members, summed, 0.0), axis=1, keepdims=True
        )
        root_term = system / scale
        middle = 1.5 * identity - 0.5 * root_term
        root[b] = split_dot(root_term, middle)
        inverse[b] = middle

    @pl.loop(0, levels_n, unroll=2)
    def _(f):
        cell = state_ref[:, f].astype(jnp.float32)
        average = jnp.sum(cell, axis=0) / members
        mean[f] = average
        dev[f] = (cell - average[None]).reshape(deep, tile_cols).astype(jnp.bfloat16)

    @pl.loop(0, ns_iters - 2)
    def _(repeat):
        for b in range(tile_rows):
            root_term, term = root[b], inverse[b]
            middle = 1.5 * identity - 0.5 * split_dot(term, root_term)
            root[b] = split_dot(root_term, middle)
            inverse[b] = split_dot(middle, term)

    chosen = lax.broadcasted_iota(jnp.int32, (members, span), 0)
    place = lax.broadcasted_iota(jnp.int32, (members, span), 1)
    picked = (place // padded_members) * group_members + lax.rem(place, padded_members)
    pick = jnp.where(
        (picked == chosen) & (lax.rem(place, padded_members) < group_members), 1.0, 0.0
    ).astype(jnp.bfloat16)
    source = lax.broadcasted_iota(jnp.int32, (span, deep), 0)
    spot = lax.broadcasted_iota(jnp.int32, (span, deep), 1)
    member_of = (source // padded_members) * group_members + lax.rem(source, padded_members)
    spot = jnp.where(
        lax.rem(source, padded_members) < group_members, spot - member_of * tile_rows, -1
    )

    for b in range(tile_rows):
        term = inverse[b]
        middle = 1.5 * identity - 0.5 * split_dot(term, root[b])
        term = split_dot(middle, term)
        scale = scales[b][:1, :1]
        half_step = jnp.sum(term * target[b], axis=0, keepdims=True)
        shift = jnp.sum(term * half_step, axis=1, keepdims=True) / scale
        spread = jnp.sqrt(jnp.float32(members - 1)) * term / jnp.sqrt(scale)
        transform = (spread + shift).astype(jnp.bfloat16)
        turned = lax.dot_general(
            pick, transform, (((1,), (1,)), ((), ())), preferred_element_type=jnp.float32
        ).astype(jnp.bfloat16)
        spread_out = jnp.dot(
            turned,
            jnp.where(spot == b, 1.0, 0.0).astype(jnp.bfloat16),
            preferred_element_type=jnp.float32,
        )
        for part in range(deep // tile_cols):
            wide[part, pl.ds(b, members, stride=tile_rows), :] = spread_out[
                :, part * tile_cols : (part + 1) * tile_cols
            ]

    for part in range(deep // tile_cols):
        big[:, part * tile_cols : (part + 1) * tile_cols] = wide[part].astype(jnp.bfloat16)

    def send(pair):
        return pltpu.make_async_copy(
            result.at[:, pl.ds(pair * 2, 2)], out_ref.at[:, pl.ds(pair * 2, 2)], out_sem.at[pair]
        )

    chunk = 128

    @pl.loop(0, levels_n // 2)
    def _(pair):
        f = pair * 2
        right = jnp.concatenate([dev[f], dev[f + 1]], axis=1)
        averages = [mean[f], mean[f + 1]]
        for first in range(0, deep, chunk):
            update = jnp.dot(
                big[first : first + chunk, :], right, preferred_element_type=jnp.float32
            )
            for half in range(2):
                block = update[:, half * tile_cols : (half + 1) * tile_cols].reshape(
                    chunk // tile_rows, tile_rows, tile_cols
                )
                result[first // tile_rows : (first + chunk) // tile_rows, f + half] = (
                    block + averages[half][None]
                ).astype(jnp.bfloat16)
        send(pair).start()

    @pl.loop(0, levels_n // 2)
    def _(pair):
        send(pair).wait()


def per_device(
    ensemble,
    obs_interp,
    obs_start,
    obs_levels,
    obs_values,
    obs_weight,
    obs_rows,
    obs_count,
    local_mask,
):
    lat_n = lax.axis_size("lat")
    lon_n = lax.axis_size("lon")
    total = lat_n * lon_n
    share, grid_rows, grid_cols = ensemble.shape
    tile_rows = grid_rows // lat_n
    tile_cols = grid_cols // lon_n
    slots_n, levels_n, obs_n = obs_levels.shape[2:]
    members = share * total // levels_n
    group = math.lcm(share, math.lcm(levels_n, 16)) // share
    groups = total // group
    group_members = group * share // levels_n
    padded_members = (group_members // 8 + 1) * 8
    span = groups * padded_members
    plan = (lat_n, lon_n, share, tile_rows, tile_cols, levels_n, members, group)
    vmem = pl.BlockSpec(memory_space=pltpu.VMEM)
    smem = pl.BlockSpec(memory_space=pltpu.SMEM)
    state, slots = pl.pallas_call(
        functools.partial(gather_kernel, plan),
        out_shape=(
            jax.ShapeDtypeStruct((share * total, tile_rows, tile_cols), jnp.bfloat16),
            jax.ShapeDtypeStruct((9, span, span), jnp.float32),
        ),
        in_specs=[pl.BlockSpec(memory_space=pltpu.HBM)] * 6 + [smem] * 2,
        out_specs=(vmem, vmem),
        scratch_shapes=[
            pltpu.VMEM(array.shape, array.dtype)
            for array in (obs_interp, obs_start, obs_levels, obs_values, obs_weight)
        ]
        + [
            pltpu.VMEM((slots_n, tile_cols, obs_n), jnp.bfloat16),
            pltpu.VMEM((tile_rows, group * share, tile_cols), jnp.bfloat16),
            pltpu.VMEM((group * share * tile_rows, tile_cols), jnp.float32),
            pltpu.VMEM((slots_n, span, obs_n), jnp.float32),
            pltpu.VMEM((span, span), jnp.float32),
            pltpu.SemaphoreType.DMA((total,)),
            pltpu.SemaphoreType.DMA((total,)),
            pltpu.SemaphoreType.DMA((9,)),
            pltpu.SemaphoreType.DMA((9,)),
            pltpu.SemaphoreType.DMA((5,)),
        ],
        compiler_params=pltpu.CompilerParams(
            collective_id=0, has_side_effects=True, vmem_limit_bytes=54 * 1024 * 1024
        ),
    )(
        ensemble,
        obs_interp,
        obs_start,
        obs_levels,
        obs_values,
        obs_weight,
        obs_rows.reshape(-1),
        obs_count.reshape(-1),
    )
    tile_state = state.reshape(members, levels_n, tile_rows, tile_cols)
    tiles = (tile_rows, span, span)
    deep = members * tile_rows
    plan = (members, levels_n, tile_rows, tile_cols, group_members, padded_members, NS_ITERS)
    return pl.pallas_call(
        functools.partial(analysis_kernel, plan),
        out_shape=jax.ShapeDtypeStruct(tile_state.shape, jnp.bfloat16),
        in_specs=[vmem, vmem, smem],
        out_specs=pl.BlockSpec(memory_space=pltpu.HBM),
        scratch_shapes=[
            pltpu.VMEM(tiles, jnp.float32),
            pltpu.VMEM(tiles, jnp.float32),
            pltpu.VMEM((tile_rows, span, 1), jnp.float32),
            pltpu.VMEM((tile_rows, 8, 128), jnp.float32),
            pltpu.VMEM((deep // tile_cols, deep, tile_cols), jnp.float32),
            pltpu.VMEM((deep, deep), jnp.bfloat16),
            pltpu.VMEM((levels_n, deep, tile_cols), jnp.bfloat16),
            pltpu.VMEM((levels_n, tile_rows, tile_cols), jnp.float32),
            pltpu.VMEM(tile_state.shape, jnp.bfloat16),
            pltpu.SemaphoreType.DMA((levels_n // 2,)),
        ],
        compiler_params=pltpu.CompilerParams(vmem_limit_bytes=40 * 1024 * 1024),
    )(tile_state, slots, local_mask.reshape(-1))


def solution(mesh):
    placed = (
        P(("lat", "lon"), None, None),
        P("lat", "lon", None, None, None),
        P("lat", "lon", None, None),
        P("lat", "lon", None, None, None),
        P("lat", "lon", None, None),
        P("lat", "lon", None, None),
        P("lat", "lon", None),
        P("lat", "lon"),
        P("lat", "lon", None, None),
    )
    return jax.shard_map(
        per_device,
        mesh=mesh,
        in_specs=placed,
        out_specs=P(None, None, "lat", "lon"),
        check_vma=False,
    )
```
